32 devices in a mesh: row: 8 (over y, x, core), col: 4 (over z).
Axes of the slice: x: 2, y: 2, z: 4, core: 2. Of those that a mesh axis runs over, the one named last changes fastest.
Arguments:
- grad_x: float32 [4096, 2048], P('row', 'col'), may hold values from -6 to 6
- grad_y: float32 [4096, 2048], P('row', 'col'), may hold values from -6 to 6
Outputs:
- field: float32 [4096, 2048], P('row', 'col')
The draws below stay inside these ranges and needn't reach their ends.
All inputs are finite; a program needn't handle non-finite values.
Results may differ from the reference program's by a relative error of at most 0.0003.
Values sent between devices are 32-bit elements; how exact they have to be, the bound alone decides.
A program may use at most 64 MiB of HBM per device.

```python
import math
import jax
import jax.numpy as jnp

NX = 4096
NY = 2048


def block_scale(key, dims, pieces, smallest, high):
    factor_of, own = 1.0, jax.random.fold_in(key, 6)
    for position, parts in pieces:
        steps = jnp.exp(jax.random.uniform(jax.random.fold_in(own, position), (parts,), jnp.float32, smallest / len(pieces), high / len(pieces)))
        factor_of = factor_of * jnp.repeat(steps, dims[position] // parts).reshape([-1 if axis == position else 1 for axis in range(len(dims))])
    return factor_of


def gaussian(rng, extent, scale, limit, pieces=(), kind=jnp.bfloat16):
    array = jax.random.normal(rng, extent, jnp.float32) * scale
    if len(pieces) > 0:
        array = block_scale(rng, extent, pieces, -0.22, 0.18) * array
    return jnp.clip(array, min=-limit, max=limit).astype(kind)


def setup_inputs(seed: int = 0) -> dict:
    splits = jax.random.split(jax.random.key(seed), 3)
    grad_x = gaussian(splits[0], (NX, NY), 1.0, 6.0, ((0, 8), (1, 4)), jnp.float32)
    grad_y = gaussian(splits[1], (NX, NY), 1.0, 6.0, ((0, 8), (1, 4)), jnp.float32)
    return dict(grad_x=grad_x, grad_y=grad_y)


def cosine_forward(values):
    length = values.shape[0]
    spec = jnp.fft.rfft(values, n=2 * length, axis=0)[:length]
    angle = jnp.arange(length, dtype=jnp.float32) * (math.pi / (2 * length))
    return jnp.cos(angle)[:, None] * spec.real + jnp.sin(angle)[:, None] * spec.imag


def cosine_inverse(values):
    length = values.shape[0]
    angle = jnp.arange(length, dtype=jnp.float32) * (math.pi / (2 * length))
    real_part = values * jnp.cos(angle)[:, None]
    imag_part = values * jnp.sin(angle)[:, None]
    zero_row = jnp.zeros((1, values.shape[1]), values.dtype)
    real_part = jnp.concatenate([2.0 * real_part[:1], real_part[1:], zero_row], 0)
    imag_part = jnp.concatenate([2.0 * imag_part[:1], imag_part[1:], zero_row], 0)
    packed = real_part + 1j * imag_part
    return jnp.fft.irfft(packed, n=2 * length, axis=0)[:length] * length


def reference(grad_x, grad_y):
    zero_row = jnp.zeros((1, grad_x.shape[1]), grad_x.dtype)
    zero_col = jnp.zeros((grad_y.shape[0], 1), grad_y.dtype)
    diverge = (grad_x - jnp.concatenate([zero_row, grad_x[:-1]], 0)) + (grad_y - jnp.concatenate([zero_col, grad_y[:, :-1]], 1))
    spectrum = cosine_forward(cosine_forward(diverge).T).T
    total_x, total_y = spectrum.shape
    freq_x = jnp.arange(total_x, dtype=jnp.float32)
    freq_y = jnp.arange(total_y, dtype=jnp.float32)
    eigen = -4.0 * jnp.sin(freq_x * (math.pi / (2 * total_x)))[:, None] ** 2 - 4.0 * jnp.sin(freq_y * (math.pi / (2 * total_y)))[None, :] ** 2
    weight_x = jnp.where(freq_x == 0, 1.0, 2.0) / total_x
    weight_y = jnp.where(freq_y == 0, 1.0, 2.0) / total_y
    anchor = (freq_x == 0)[:, None] & (freq_y == 0)[None, :]
    scaled = jnp.where(anchor, 0.0, spectrum / jnp.where(anchor, 1.0, eigen)) * weight_x[:, None] * weight_y[None, :]
    return cosine_inverse(cosine_inverse(scaled).T).T
```

```python
import functools

import jax
import jax.numpy as jnp
import numpy as np
from jax import lax
from jax.experimental import pallas as pl
from jax.experimental.pallas import tpu as pltpu
from jax.sharding import PartitionSpec as P

MESH = pl.DeviceIdType.MESH
LANES = 128


def split3(values):
    first = values.astype(jnp.bfloat16)
    rest = values - first.astype(jnp.float32)
    second = rest.astype(jnp.bfloat16)
    third = (rest - second.astype(jnp.float32)).astype(jnp.bfloat16)
    return first, second, third


def tables(n, cols_members, length, breadth):
    total_x, total_y, chunk, half = n * length, cols_members * breadth, breadth // n, length // 2
    place = np.arange(length)[:, None]
    level = np.arange(half)[None, :]
    phase = ((2 * place + 1) * level) % (2 * length) * (np.pi / length)
    cosine, sine = np.cos(phase), np.sin(phase)
    sine[:, 0] = (-1.0) ** np.arange(length)

    def pieces(table):
        table = table.astype(np.float32)
        kept = []
        for _ in range(3):
            part = table.astype(jnp.bfloat16)
            kept.append(part)
            table = table - part.astype(np.float32)
        return np.stack(kept)

    twist = np.pi * np.arange(n + 1)[:, None] * (2 * np.arange(length)[None, :] + 1) / (2 * total_x)
    turn = np.stack([np.cos(twist), np.sin(twist)]).astype(np.float32)
    freq = np.concatenate(
        [
            np.arange(n + 1)[:, None] + 2 * n * level,
            2 * n * np.where(level == 0, half, level) - np.arange(1, n)[:, None],
        ]
    )
    s = np.sin(np.pi * freq / (2 * total_x))
    c = np.sqrt(1 + s * s)
    zero = freq == 0
    rate = -2 * np.log(c + s)
    decay = lambda count: np.exp(rate * count)
    closing = np.where(zero, 1.0, -np.expm1(np.where(zero, -1.0, rate) * 2 * total_y))
    gain = np.where(zero, 0.0, -2.0 / total_x / np.where(zero, 1.0, 4 * c * s))
    solve = np.stack(
        [
            -np.expm1(rate),
            decay(chunk),
            decay(breadth),
            decay(total_y),
            1 / closing,
            gain,
        ]
    ).astype(np.float32)
    return pieces(cosine), pieces(sine), turn, solve


def weighted(terms):
    total = None
    for coefficient, value in terms:
        if abs(coefficient) < 1e-12:
            continue
        if abs(abs(coefficient) - 1) < 1e-12:
            if total is None:
                total = value if coefficient > 0 else -value
            else:
                total = total + value if coefficient > 0 else total - value
            continue
        part = float(coefficient) * value
        total = part if total is None else total + part
    return total


def kernel(
    n, m, gx, gy, cos3, sin3, turn, solve, out,
    dt, recv, hx, hys, hy, s_ref, t_ref, f_ref, u_ref, m1s, m1r, m2s, m2r, sh, th, ob, ot,
    hsend, hrecv, a_send, a_recv, b_send, b_recv, c_send, c_recv, d_send, d_recv,
):
    r, c = lax.axis_index("row"), lax.axis_index("col")
    length, breadth = gx.shape
    chunk, half = breadth // n, length // 2
    tiles, classes = half // LANES, 2 * n
    total_x, total_y = n * length, m * breadth

    barrier = pltpu.get_barrier_semaphore()
    for t in range(1, n):
        pl.semaphore_signal(barrier, inc=1, device_id={"row": lax.rem(r + t, n)}, device_id_type=MESH)
    for t in range(1, m):
        pl.semaphore_signal(barrier, inc=1, device_id={"col": lax.rem(c + t, m)}, device_id_type=MESH)
    pl.semaphore_wait(barrier, n - 1 + m - 1)

    def remote(src, dst, send, recv_sem, axis, who):
        return pltpu.make_async_remote_copy(
            src_ref=src, dst_ref=dst, send_sem=send, recv_sem=recv_sem,
            device_id={axis: who}, device_id_type=MESH,
        )

    halo_x = remote(gx.at[pl.ds(length - 8, 8)], hx, hsend.at[0], hrecv.at[0], "row", lax.rem(r + 1, n))
    halo_x.start()
    hys[...] = gy[:, breadth - LANES:].T[LANES - 8:]
    halo_y = remote(hys, hy, hsend.at[1], hrecv.at[1], "col", lax.rem(c + 1, m))
    halo_y.start()
    halo_x.wait()
    above = hx[7:8, :] * jnp.where(r > 0, 1.0, 0.0)
    lane = lax.broadcasted_iota(jnp.int32, (length, LANES), 1)
    line = lax.broadcasted_iota(jnp.int32, (length, LANES), 0)
    for g in range(breadth // LANES):
        here = slice(g * LANES, (g + 1) * LANES)
        x = gx[:, here]
        up = jnp.where(line == 0, above[:, here], pltpu.roll(x, 1, 0))
        y = gy[:, here]
        edge = pltpu.roll(gy[:, (g - 1) * LANES: g * LANES], 1, 1) if g else 0.0
        left = jnp.where(lane == 0, edge, pltpu.roll(y, 1, 1))
        dt[here, :] = ((x - up) + (y - left)).T
    halo_y.wait()
    top = lax.broadcasted_iota(jnp.int32, (8, length), 0) == 0
    dt[0:8, :] = dt[0:8, :] - jnp.where(top, hy[7:8, :] * jnp.where(c > 0, 1.0, 0.0), 0.0)

    copies = []
    for t in range(1, n):
        who = lax.rem(r + t, n)
        copy = remote(
            dt.at[pl.ds(pl.multiple_of(who * chunk, chunk), chunk)], recv.at[r],
            a_send.at[t], a_recv.at[t], "row", who,
        )
        copy.start()
        copies.append(copy)
    recv[r] = dt[pl.ds(pl.multiple_of(r * chunk, chunk), chunk), :]
    for copy in copies:
        copy.wait()

    step = 16
    ccos = [[np.cos(np.pi * d * p / n) for p in range(n)] for d in range(n + 1)]
    csin = [[np.sin(np.pi * d * p / n) for p in range(n)] for d in range(n + 1)]

    def mix(b, carry):
        rows = pl.ds(pl.multiple_of(b * step, step), step)
        for g in range(length // LANES):
            here = slice(g * LANES, (g + 1) * LANES)
            x = [recv[p, rows, here] for p in range(n)]
            plus = {p: x[p] + x[n - p] for p in range(1, n // 2)}
            minus = {p: x[p] - x[n - p] for p in range(1, n // 2)}
            for d in range(n + 1):
                even = d % 2 == 0
                base = [(1.0, x[0]), (ccos[d][n // 2], x[n // 2])]
                pair, other = (plus, minus) if even else (minus, plus)
                real = weighted(base + [(ccos[d][p], pair[p]) for p in pair])
                imag = weighted([(csin[d][n // 2], x[n // 2])] + [(csin[d][p], other[p]) for p in other])
                own = pl.ds(pl.multiple_of(d * chunk + b * step, step), step)
                if d == 0:
                    s_val = real
                else:
                    co, si = turn[0, d:d + 1, here], turn[1, d:d + 1, here]
                    s_val = co * real if imag is None else co * real - si * imag
                    t_val = si * real if imag is None else si * real + co * imag
                    prior = pl.ds(pl.multiple_of((d - 1) * chunk + b * step, step), step)
                    for i, part in enumerate(split3(t_val)):
                        t_ref[i, prior, here] = part
                for i, part in enumerate(split3(s_val)):
                    s_ref[i, own, here] = part
        return carry

    lax.fori_loop(0, chunk // step, mix, 0)

    def six(a, b):
        dot = functools.partial(jnp.dot, preferred_element_type=jnp.float32)
        small = dot(a[2], b[0]) + dot(a[1], b[1]) + dot(a[0], b[2])
        return dot(a[0], b[0]) + (dot(a[1], b[0]) + dot(a[0], b[1]) + small)

    mask = jnp.where(lax.broadcasted_iota(jnp.int32, (chunk, LANES), 1) == 0, 0.0, 1.0)

    def class_rows(k):
        return pl.ds(pl.multiple_of(k * chunk, chunk), chunk)

    for h in range(tiles):
        there = slice(h * LANES, (h + 1) * LANES)
        p_all = six([s_ref[i] for i in range(3)], [cos3[i, :, there] for i in range(3)])
        q_all = six([t_ref[i] for i in range(3)], [sin3[i, :, there] for i in range(3)])
        f_ref[h, 0:chunk, :] = p_all[0:chunk]
        for d in range(1, n + 1):
            pd, qd = p_all[d * chunk:(d + 1) * chunk], q_all[(d - 1) * chunk: d * chunk]
            f_ref[h, d * chunk:(d + 1) * chunk, :] = pd - (mask * qd if h == 0 else qd)
            if d < n:
                f_ref[h, (n + d) * chunk:(n + d + 1) * chunk, :] = (mask * pd if h == 0 else pd) + qd

    span = lambda i, h: solve[i, :, h * LANES:(h + 1) * LANES]
    fall = [span(0, h) for h in range(tiles)]
    at = lambda j: pl.ds(j, classes, stride=chunk)

    def sums(j, carry):
        ahead, back = carry
        new_ahead, new_back = [], []
        for h in range(tiles):
            new_ahead.append((ahead[h] - fall[h] * ahead[h]) + f_ref[h, at(j), :])
            new_back.append((back[h] - fall[h] * back[h]) + f_ref[h, at(chunk - 1 - j), :])
        return new_ahead, new_back

    nothing = [jnp.zeros((classes, LANES), jnp.float32) for _ in range(tiles)]
    ahead, back = lax.fori_loop(0, chunk, sums, (nothing, nothing))
    for h in range(tiles):
        there = slice(h * LANES, (h + 1) * LANES)
        m1s[0:classes, there] = ahead[h]
        m1s[classes:2 * classes, there] = back[h]
    m1s[2 * classes:, :] = jnp.zeros((8, half), jnp.float32)
    m1s[2 * classes:2 * classes + 1, 0:chunk] = f_ref[0, 0:chunk, :].T[0:1, :]
    copies = []
    for t in range(1, n):
        copy = remote(m1s, m1r.at[r], b_send.at[t], b_recv.at[t], "row", lax.rem(r + t, n))
        copy.start()
        copies.append(copy)
    m1r[r] = m1s[...]
    for copy in copies:
        copy.wait()
    grow = solve[1]
    band_a = jnp.zeros((classes, half), jnp.float32)
    band_b = jnp.zeros((classes, half), jnp.float32)
    for p in range(n):
        band_a = grow * band_a + m1r[p, 0:classes, :]
        band_b = grow * band_b + m1r[n - 1 - p, classes:2 * classes, :]
    m2s[0:classes, :] = band_a
    m2s[classes:2 * classes, :] = band_b
    for p in range(n):
        m2s[2 * classes + p:2 * classes + p + 1, :] = m1r[p, 2 * classes:2 * classes + 1, :]
    copies = []
    for t in range(1, m):
        copy = remote(m2s, m2r.at[c], c_send.at[t], c_recv.at[t], "col", lax.rem(c + t, m))
        copy.start()
        copies.append(copy)
    m2r[c] = m2s[...]
    for copy in copies:
        copy.wait()

    wide, whole, close = solve[2], solve[3], solve[4]
    first = jnp.zeros((classes, half), jnp.float32)
    last = jnp.zeros((classes, half), jnp.float32)
    for q in range(m):
        last = wide * last + m2r[q, 0:classes, :]
        first = wide * first + m2r[m - 1 - q, classes:2 * classes, :]
    left_in = (first + whole * last) * close
    right_in = (last + whole * first) * close
    for q in range(m):
        left_in = jnp.where(q < c, wide * left_in + m2r[q, 0:classes, :], left_in)
        right_in = jnp.where(m - 1 - q > c, wide * right_in + m2r[m - 1 - q, classes:2 * classes, :], right_in)
    for p in range(n):
        left_in = jnp.where(p < r, grow * left_in + m1r[p, 0:classes, :], left_in)
        right_in = jnp.where(n - 1 - p > r, grow * right_in + m1r[n - 1 - p, classes:2 * classes, :], right_in)

    me = lax.broadcasted_iota(jnp.int32, (chunk, LANES), 0) + (c * breadth + r * chunk)
    mine = me.astype(jnp.float32)
    mine_sq = mine * (mine + 1.0) * (0.5 / total_y) + (
        (total_y - 1) / 2 - (total_y * total_y - 1) / (6 * total_y)
    )
    column = lax.broadcasted_iota(jnp.int32, (1, LANES), 1).astype(jnp.float32)
    flat = jnp.zeros((chunk, LANES), jnp.float32)
    for q in range(m):
        for p in range(n):
            other = column + float(q * breadth + p * chunk)
            other_sq = other * (other + 1.0) * (0.5 / total_y)
            row = m2r[q, 2 * classes + p:2 * classes + p + 1, 0:LANES]
            flat = flat + (mine_sq + other_sq - jnp.maximum(mine, other)) * row
    constant = jnp.sum(flat, axis=1, keepdims=True) * (-1.0 / total_x)

    gain = [span(5, h) for h in range(tiles)]

    def forth(j, ahead):
        new = []
        for h in range(tiles):
            value = (ahead[h] - fall[h] * ahead[h]) + f_ref[h, at(j), :]
            u_ref[h, at(j), :] = value
            new.append(value)
        return new

    def backward(i, back):
        j = chunk - 1 - i
        new = []
        for h in range(tiles):
            kept = back[h] - fall[h] * back[h]
            u_ref[h, at(j), :] = gain[h] * (u_ref[h, at(j), :] + kept)
            new.append(kept + f_ref[h, at(j), :])
        return new

    parts = lambda v: [v[:, h * LANES:(h + 1) * LANES] for h in range(tiles)]
    lax.fori_loop(0, chunk, forth, parts(left_in))
    lax.fori_loop(0, chunk, backward, parts(right_in))
    u_ref[0, 0:chunk, :] = jnp.where(mask == 0.0, constant, u_ref[0, 0:chunk, :])

    for h in range(tiles):
        there = slice(h * LANES, (h + 1) * LANES)
        for d in range(n + 1):
            up = u_ref[h, d * chunk:(d + 1) * chunk, :]
            held = mask * up if h == 0 else up
            if 0 < d < n:
                um = u_ref[h, (n + d) * chunk:(n + d + 1) * chunk, :]
                pd, qd = up + (mask * um if h == 0 else um), um - held
            else:
                pd, qd = up, -held
            for i, part in enumerate(split3(pd)[:2]):
                s_ref[i, d * chunk:(d + 1) * chunk, there] = part
            if d > 0:
                for i, part in enumerate(split3(qd)[:2]):
                    t_ref[i, (d - 1) * chunk: d * chunk, there] = part

    def three(a, table, here):
        dot = lambda x, y: lax.dot_general(
            x, y, (((1,), (1,)), ((), ())), preferred_element_type=jnp.float32
        )
        b = [table[i, here, :] for i in range(2)]
        return dot(a[0], b[0]) + (dot(a[1], b[0]) + dot(a[0], b[1]))

    for g in range(length // 256):
        here = slice(g * 256, (g + 1) * 256)
        sh[:, here] = three([s_ref[i, :, 0:half] for i in range(2)], cos3, here)
        th[:, here] = three([t_ref[i, :, 0:half] for i in range(2)], sin3, here)

    def unmix(b, carry):
        for g in range(length // LANES):
            here = slice(g * LANES, (g + 1) * LANES)
            step = 8
            rows = pl.ds(pl.multiple_of(b * step, step), step)
            real, imag = [], []
            for d in range(n + 1):
                s_val = sh[pl.ds(pl.multiple_of(d * chunk + b * step, step), step), here]
                if d == 0:
                    real.append(s_val)
                    imag.append(None)
                    continue
                t_val = th[pl.ds(pl.multiple_of((d - 1) * chunk + b * step, step), step), here]
                co, si = turn[0, d:d + 1, here], turn[1, d:d + 1, here]
                real.append(co * s_val + si * t_val)
                imag.append(co * t_val - si * s_val)
            for p in range(n // 2 + 1):
                evens = weighted([(ccos[d][p], real[d]) for d in range(0, n + 1, 2)])
                odds = weighted([(ccos[d][p], real[d]) for d in range(1, n + 1, 2)])
                if p == 0:
                    ob[0, rows, here] = evens + odds
                    continue
                ievens = weighted([(csin[d][p], imag[d]) for d in range(2, n, 2)])
                iodds = weighted([(csin[d][p], imag[d]) for d in range(1, n, 2)])
                if p == n // 2:
                    ob[p, rows, here] = weighted(
                        [(1.0, v) for v in (evens, odds, ievens, iodds) if v is not None]
                    )
                    continue
                near, far = evens + iodds, odds + ievens
                ob[p, rows, here] = near + far
                ob[n - p, rows, here] = (evens - ievens) + (iodds - odds)
        return carry

    lax.fori_loop(0, chunk // 8, unmix, 0)
    copies = []
    home = pl.ds(pl.multiple_of(r * chunk, chunk), chunk)
    for t in range(1, n):
        who = lax.rem(r + t, n)
        copy = remote(ob.at[who], ot.at[home], d_send.at[t], d_recv.at[t], "row", who)
        copy.start()
        copies.append(copy)
    ot[home, :] = ob[r]
    for copy in copies:
        copy.wait()
    for g in range(breadth // LANES):
        here = slice(g * LANES, (g + 1) * LANES)
        out[:, here] = ot[here, :].T


def body(grad_x, grad_y):
    n, m = lax.axis_size("row"), lax.axis_size("col")
    length, breadth = grad_x.shape
    chunk, half, classes = breadth // n, length // 2, 2 * n
    constants = tables(n, m, length, breadth)
    f32, bf16 = jnp.float32, jnp.bfloat16
    size1, size2 = 2 * classes + 8, 2 * classes + -(-n // 8) * 8
    dma = pltpu.SemaphoreType.DMA
    return pl.pallas_call(
        functools.partial(kernel, n, m),
        out_shape=jax.ShapeDtypeStruct((length, breadth), f32),
        in_specs=[pl.BlockSpec(memory_space=pltpu.VMEM)] * 6,
        out_specs=pl.BlockSpec(memory_space=pltpu.VMEM),
        scratch_shapes=[
            pltpu.VMEM((breadth, length), f32),
            pltpu.VMEM((n, chunk, length), f32),
            pltpu.VMEM((8, breadth), f32),
            pltpu.VMEM((8, length), f32),
            pltpu.VMEM((8, length), f32),
            pltpu.VMEM((3, (n + 1) * chunk, length), bf16),
            pltpu.VMEM((3, n * chunk, length), bf16),
            pltpu.VMEM((half // LANES, classes * chunk, LANES), f32),
            pltpu.VMEM((half // LANES, classes * chunk, LANES), f32),
            pltpu.VMEM((size1, half), f32),
            pltpu.VMEM((n, size1, half), f32),
            pltpu.VMEM((size2, half), f32),
            pltpu.VMEM((m, size2, half), f32),
            pltpu.VMEM(((n + 1) * chunk, length), f32),
            pltpu.VMEM((n * chunk, length), f32),
            pltpu.VMEM((n, chunk, length), f32),
            pltpu.VMEM((breadth, length), f32),
            dma((2,)), dma((2,)),
            dma((n,)), dma((n,)), dma((n,)), dma((n,)),
            dma((m,)), dma((m,)), dma((n,)), dma((n,)),
        ],
        compiler_params=pltpu.CompilerParams(
            collective_id=0, has_side_effects=True, vmem_limit_bytes=60 * 1024 * 1024
        ),
        name="poisson",
    )(grad_x, grad_y, *[jnp.asarray(value) for value in constants])


def solution(mesh):
    placed = (P("row", "col"), P("row", "col"))
    return jax.shard_map(
        body, mesh=mesh, in_specs=placed, out_specs=P("row", "col"), check_vma=False
    )
```

```python
import functools

import jax
import jax.numpy as jnp
import numpy as np
from jax import lax
from jax.experimental import pallas as pl
from jax.experimental.pallas import tpu as pltpu
from jax.sharding import PartitionSpec as P

MESH = pl.DeviceIdType.MESH
LANES = 128


def split3(values):
    first = values.astype(jnp.bfloat16)
    rest = values - first.astype(jnp.float32)
    second = rest.astype(jnp.bfloat16)
    third = (rest - second.astype(jnp.float32)).astype(jnp.bfloat16)
    return first, second, third


def tables(n, cols_members, length, breadth):
    total_x, total_y, chunk, half = n * length, cols_members * breadth, breadth // n, length // 2
    place = np.arange(length)[:, None]
    level = np.arange(half)[None, :]
    phase = ((2 * place + 1) * level) % (2 * length) * (np.pi / length)
    cosine, sine = np.cos(phase), np.sin(phase)
    sine[:, 0] = (-1.0) ** np.arange(length)

    def pieces(table):
        table = table.astype(np.float32)
        kept = []
        for _ in range(3):
            part = table.astype(jnp.bfloat16)
            kept.append(part)
            table = table - part.astype(np.float32)
        return np.stack(kept)

    twist = np.pi * np.arange(n + 1)[:, None] * (2 * np.arange(length)[None, :] + 1) / (2 * total_x)
    turn = np.stack([np.cos(twist), np.sin(twist)]).astype(np.float32)
    freq = np.concatenate(
        [
            np.arange(n + 1)[:, None] + 2 * n * level,
            2 * n * np.where(level == 0, half, level) - np.arange(1, n)[:, None],
        ]
    )
    s = np.sin(np.pi * freq / (2 * total_x))
    c = np.sqrt(1 + s * s)
    zero = freq == 0
    rate = -2 * np.log(c + s)
    decay = lambda count: np.exp(rate * count)
    closing = np.where(zero, 1.0, -np.expm1(np.where(zero, -1.0, rate) * 2 * total_y))
    gain = np.where(zero, 0.0, -2.0 / total_x / np.where(zero, 1.0, 4 * c * s))
    solve = np.stack(
        [
            -np.expm1(rate),
            decay(chunk),
            decay(breadth),
            decay(total_y),
            1 / closing,
            gain,
        ]
    ).astype(np.float32)
    return pieces(cosine), pieces(sine), turn, solve


def weighted(terms):
    total = None
    for coefficient, value in terms:
        if abs(coefficient) < 1e-12:
            continue
        if abs(abs(coefficient) - 1) < 1e-12:
            if total is None:
                total = value if coefficient > 0 else -value
            else:
                total = total + value if coefficient > 0 else total - value
            continue
        part = float(coefficient) * value
        total = part if total is None else total + part
    return total


def kernel(
    n, m, gx, gy, cos3, sin3, turn, solve, out,
    dt, recv, hx, hys, hy, s_ref, t_ref, f_ref, u_ref, m1s, m1r, m2s, m2r, sh, th, ob, ot,
    hsend, hrecv, a_send, a_recv, b_send, b_recv, c_send, c_recv, d_send, d_recv,
):
    r, c = lax.axis_index("row"), lax.axis_index("col")
    length, breadth = gx.shape
    chunk, half = breadth // n, length // 2
    tiles, classes = half // LANES, 2 * n
    total_x, total_y = n * length, m * breadth

    barrier = pltpu.get_barrier_semaphore()
    for t in range(1, n):
        pl.semaphore_signal(barrier, inc=1, device_id={"row": lax.rem(r + t, n)}, device_id_type=MESH)
    for t in range(1, m):
        pl.semaphore_signal(barrier, inc=1, device_id={"col": lax.rem(c + t, m)}, device_id_type=MESH)
    pl.semaphore_wait(barrier, n - 1 + m - 1)

    def remote(src, dst, send, recv_sem, axis, who):
        return pltpu.make_async_remote_copy(
            src_ref=src, dst_ref=dst, send_sem=send, recv_sem=recv_sem,
            device_id={axis: who}, device_id_type=MESH,
        )

    halo_x = remote(gx.at[pl.ds(length - 8, 8)], hx, hsend.at[0], hrecv.at[0], "row", lax.rem(r + 1, n))
    halo_x.start()
    hys[...] = gy[:, breadth - LANES:].T[LANES - 8:]
    halo_y = remote(hys, hy, hsend.at[1], hrecv.at[1], "col", lax.rem(c + 1, m))
    halo_y.start()
    halo_x.wait()
    above = hx[7:8, :] * jnp.where(r > 0, 1.0, 0.0)
    lane = lax.broadcasted_iota(jnp.int32, (length, LANES), 1)
    line = lax.broadcasted_iota(jnp.int32, (length, LANES), 0)
    for g in range(breadth // LANES):
        here = slice(g * LANES, (g + 1) * LANES)
        x = gx[:, here]
        up = jnp.where(line == 0, above[:, here], pltpu.roll(x, 1, 0))
        y = gy[:, here]
        edge = pltpu.roll(gy[:, (g - 1) * LANES: g * LANES], 1, 1) if g else 0.0
        left = jnp.where(lane == 0, edge, pltpu.roll(y, 1, 1))
        dt[here, :] = ((x - up) + (y - left)).T
    halo_y.wait()
    top = lax.broadcasted_iota(jnp.int32, (8, length), 0) == 0
    dt[0:8, :] = dt[0:8, :] - jnp.where(top, hy[7:8, :] * jnp.where(c > 0, 1.0, 0.0), 0.0)

    step = 16
    rounds = chunk // step

    def out_piece(i, t):
        who = lax.rem(r + t, n)
        source = pl.multiple_of(who * chunk + i * step, step)
        return remote(
            dt.at[pl.ds(source, step)], recv.at[r, pl.ds(pl.multiple_of(i * step, step), step)],
            a_send.at[i, t], a_recv.at[i, t], "row", who,
        )

    def send_out(i, carry):
        for t in range(1, n):
            out_piece(i, t).start()
        return carry

    lax.fori_loop(0, rounds, send_out, 0)
    recv[r] = dt[pl.ds(pl.multiple_of(r * chunk, chunk), chunk), :]

    depth_s, depth_t = (n + 1) * step, n * step
    ccos = [[np.cos(np.pi * d * p / n) for p in range(n)] for d in range(n + 1)]
    csin = [[np.sin(np.pi * d * p / n) for p in range(n)] for d in range(n + 1)]
    mask = jnp.where(lax.broadcasted_iota(jnp.int32, (step, LANES), 1) == 0, 0.0, 1.0)
    span = lambda i, h: solve[i, :, h * LANES:(h + 1) * LANES]
    fall = [span(0, h) for h in range(tiles)]
    at = lambda j: pl.ds(j, classes, stride=chunk)

    def class_rows(k, i):
        return pl.ds(pl.multiple_of(k * chunk + i * step, step), step)

    def mix(b):
        rows = pl.ds(pl.multiple_of(b * step, step), step)
        for g in range(length // LANES):
            here = slice(g * LANES, (g + 1) * LANES)
            x = [recv[p, rows, here] for p in range(n)]
            plus = {p: x[p] + x[n - p] for p in range(1, n // 2)}
            minus = {p: x[p] - x[n - p] for p in range(1, n // 2)}
            for d in range(n + 1):
                even = d % 2 == 0
                base = [(1.0, x[0]), (ccos[d][n // 2], x[n // 2])]
                pair, other = (plus, minus) if even else (minus, plus)
                real = weighted(base + [(ccos[d][p], pair[p]) for p in pair])
                imag = weighted([(csin[d][n // 2], x[n // 2])] + [(csin[d][p], other[p]) for p in other])
                if d == 0:
                    s_val = real
                else:
                    co, si = turn[0, d:d + 1, here], turn[1, d:d + 1, here]
                    s_val = co * real if imag is None else co * real - si * imag
                    t_val = si * real if imag is None else si * real + co * imag
                    for i, part in enumerate(split3(t_val)):
                        t_ref[i * depth_t + (d - 1) * step:i * depth_t + d * step, here] = part
                for i, part in enumerate(split3(s_val)):
                    s_ref[i * depth_s + d * step:i * depth_s + (d + 1) * step, here] = part

    def six(a, depth, b):
        dot = functools.partial(jnp.dot, preferred_element_type=jnp.float32)
        one = dot(a[...], b[0])
        two = dot(a[0:2 * depth], b[1])
        small = one[2 * depth:] + two[depth:] + dot(a[0:depth], b[2])
        return one[0:depth] + (one[depth:2 * depth] + two[0:depth] + small)

    def forward(i, carry):
        for t in range(1, n):
            out_piece(i, t).wait_recv()
        mix(i)
        p_all = six(s_ref, depth_s, cos3)
        q_all = six(t_ref, depth_t, sin3)
        for h in range(tiles):
            there = slice(h * LANES, (h + 1) * LANES)
            f_ref[h, class_rows(0, i), :] = p_all[0:step, there]
            for d in range(1, n + 1):
                pd, qd = p_all[d * step:(d + 1) * step, there], q_all[(d - 1) * step:d * step, there]
                f_ref[h, class_rows(d, i), :] = pd - (mask * qd if h == 0 else qd)
                if d < n:
                    f_ref[h, class_rows(n + d, i), :] = (mask * pd if h == 0 else pd) + qd
        ahead, back, power = carry
        for k in range(step):
            f = [f_ref[h, at(i * step + k), :] for h in range(tiles)]
            back = [back[h] + power[h] * f[h] for h in range(tiles)]
            power = [power[h] - fall[h] * power[h] for h in range(tiles)]
            ahead = [(ahead[h] + f[h]) - fall[h] * ahead[h] for h in range(tiles)]
        return ahead, back, power

    nothing = [jnp.zeros((classes, LANES), jnp.float32) for _ in range(tiles)]
    unity = [jnp.ones((classes, LANES), jnp.float32) for _ in range(tiles)]
    ahead, back, _ = lax.fori_loop(0, rounds, forward, (nothing, nothing, unity))
    for h in range(tiles):
        there = slice(h * LANES, (h + 1) * LANES)
        m1s[0:classes, there] = ahead[h]
        m1s[classes:2 * classes, there] = back[h]
    m1s[2 * classes:, :] = jnp.zeros((8, half), jnp.float32)
    m1s[2 * classes:2 * classes + 1, 0:chunk] = f_ref[0, 0:chunk, :].T[0:1, :]
    copies = []
    for t in range(1, n):
        copy = remote(m1s, m1r.at[r], b_send.at[t], b_recv.at[t], "row", lax.rem(r + t, n))
        copy.start()
        copies.append(copy)
    m1r[r] = m1s[...]
    for copy in copies:
        copy.wait()
    grow = solve[1]
    band_a = jnp.zeros((classes, half), jnp.float32)
    band_b = jnp.zeros((classes, half), jnp.float32)
    for p in range(n):
        band_a = grow * band_a + m1r[p, 0:classes, :]
        band_b = grow * band_b + m1r[n - 1 - p, classes:2 * classes, :]
    m2s[0:classes, :] = band_a
    m2s[classes:2 * classes, :] = band_b
    for p in range(n):
        m2s[2 * classes + p:2 * classes + p + 1, :] = m1r[p, 2 * classes:2 * classes + 1, :]
    copies = []
    for t in range(1, m):
        copy = remote(m2s, m2r.at[c], c_send.at[t], c_recv.at[t], "col", lax.rem(c + t, m))
        copy.start()
        copies.append(copy)
    m2r[c] = m2s[...]
    for copy in copies:
        copy.wait()

    wide, whole, close = solve[2], solve[3], solve[4]
    first = jnp.zeros((classes, half), jnp.float32)
    last = jnp.zeros((classes, half), jnp.float32)
    for q in range(m):
        last = wide * last + m2r[q, 0:classes, :]
        first = wide * first + m2r[m - 1 - q, classes:2 * classes, :]
    left_in = (first + whole * last) * close
    right_in = (last + whole * first) * close
    for q in range(m):
        left_in = jnp.where(q < c, wide * left_in + m2r[q, 0:classes, :], left_in)
        right_in = jnp.where(m - 1 - q > c, wide * right_in + m2r[m - 1 - q, classes:2 * classes, :], right_in)
    for p in range(n):
        left_in = jnp.where(p < r, grow * left_in + m1r[p, 0:classes, :], left_in)
        right_in = jnp.where(n - 1 - p > r, grow * right_in + m1r[n - 1 - p, classes:2 * classes, :], right_in)

    me = lax.broadcasted_iota(jnp.int32, (chunk, LANES), 0) + (c * breadth + r * chunk)
    mine = me.astype(jnp.float32)
    mine_sq = mine * (mine + 1.0) * (0.5 / total_y) + (
        (total_y - 1) / 2 - (total_y * total_y - 1) / (6 * total_y)
    )
    column = lax.broadcasted_iota(jnp.int32, (1, LANES), 1).astype(jnp.float32)
    flat = jnp.zeros((chunk, LANES), jnp.float32)
    for q in range(m):
        for p in range(n):
            other = column + float(q * breadth + p * chunk)
            other_sq = other * (other + 1.0) * (0.5 / total_y)
            row = m2r[q, 2 * classes + p:2 * classes + p + 1, 0:LANES]
            flat = flat + (mine_sq + other_sq - jnp.maximum(mine, other)) * row
    constant = jnp.sum(flat, axis=1, keepdims=True) * (-1.0 / total_x)

    gain = [span(5, h) for h in range(tiles)]

    unroll = 8

    def walk(joined):
        def some(b, carry):
            ahead, back = carry
            for k in range(unroll):
                i = b * unroll + k
                j = chunk - 1 - i
                new_ahead, new_back = [], []
                for h in range(tiles):
                    value = (ahead[h] + f_ref[h, at(i), :]) - fall[h] * ahead[h]
                    kept = back[h] - fall[h] * back[h]
                    new_ahead.append(value)
                    new_back.append((back[h] + f_ref[h, at(j), :]) - fall[h] * back[h])
                    if joined:
                        value = gain[h] * (value + u_ref[h, at(i), :])
                        kept = gain[h] * (kept + u_ref[h, at(j), :])
                    u_ref[h, at(i), :] = value
                    u_ref[h, at(j), :] = kept
                ahead, back = new_ahead, new_back
            return ahead, back

        return some

    parts = lambda v: [v[:, h * LANES:(h + 1) * LANES] for h in range(tiles)]
    middle = chunk // 2 // unroll
    state = lax.fori_loop(0, middle, walk(False), (parts(left_in), parts(right_in)))
    lax.fori_loop(middle, 2 * middle, walk(True), state)
    wide_lane = lax.broadcasted_iota(jnp.int32, (chunk, LANES), 1)
    u_ref[0, 0:chunk, :] = jnp.where(wide_lane == 0, constant, u_ref[0, 0:chunk, :])

    def three(a, depth, table):
        dot = lambda x, y: lax.dot_general(
            x, y, (((1,), (1,)), ((), ())), preferred_element_type=jnp.float32
        )
        one = dot(a[0:2 * depth, 0:half], table[0])
        return one[0:depth] + (one[depth:] + dot(a[0:depth, 0:half], table[1]))

    def back_piece(i, t):
        who = lax.rem(r + t, n)
        rows = pl.ds(pl.multiple_of(i * step, step), step)
        home = pl.ds(pl.multiple_of(r * chunk + i * step, step), step)
        return remote(
            ob.at[who, rows], ot.at[home], d_send.at[i, t], d_recv.at[i, t], "row", who
        )

    def inverse(i, carry):
        for h in range(tiles):
            there = slice(h * LANES, (h + 1) * LANES)
            for d in range(n + 1):
                up = u_ref[h, class_rows(d, i), :]
                held = mask * up if h == 0 else up
                if 0 < d < n:
                    um = u_ref[h, class_rows(n + d, i), :]
                    pd, qd = up + (mask * um if h == 0 else um), um - held
                else:
                    pd, qd = up, -held
                for k, part in enumerate(split3(pd)[:2]):
                    s_ref[k * depth_s + d * step:k * depth_s + (d + 1) * step, there] = part
                if d > 0:
                    for k, part in enumerate(split3(qd)[:2]):
                        t_ref[k * depth_t + (d - 1) * step:k * depth_t + d * step, there] = part
        sh[...] = three(s_ref, depth_s, cos3)
        th[...] = three(t_ref, depth_t, sin3)
        rows = pl.ds(pl.multiple_of(i * step, step), step)
        for g in range(length // LANES):
            here = slice(g * LANES, (g + 1) * LANES)
            real, imag = [], []
            for d in range(n + 1):
                s_val = sh[d * step:(d + 1) * step, here]
                if d == 0:
                    real.append(s_val)
                    imag.append(None)
                    continue
                t_val = th[(d - 1) * step:d * step, here]
                co, si = turn[0, d:d + 1, here], turn[1, d:d + 1, here]
                real.append(co * s_val + si * t_val)
                imag.append(co * t_val - si * s_val)
            for p in range(n // 2 + 1):
                evens = weighted([(ccos[d][p], real[d]) for d in range(0, n + 1, 2)])
                odds = weighted([(ccos[d][p], real[d]) for d in range(1, n + 1, 2)])
                if p == 0:
                    ob[0, rows, here] = evens + odds
                    continue
                ievens = weighted([(csin[d][p], imag[d]) for d in range(2, n, 2)])
                iodds = weighted([(csin[d][p], imag[d]) for d in range(1, n, 2)])
                if p == n // 2:
                    ob[p, rows, here] = weighted(
                        [(1.0, v) for v in (evens, odds, ievens, iodds) if v is not None]
                    )
                    continue
                near, far = evens + iodds, odds + ievens
                ob[p, rows, here] = near + far
                ob[n - p, rows, here] = (evens - ievens) + (iodds - odds)
        for t in range(1, n):
            back_piece(i, t).start()
        return carry

    lax.fori_loop(0, rounds, inverse, 0)
    ot[pl.ds(pl.multiple_of(r * chunk, chunk), chunk), :] = ob[r]

    def settle(i, carry):
        for t in range(1, n):
            out_piece(i, t).wait_send()
            back_piece(i, t).wait()
        return carry

    lax.fori_loop(0, rounds, settle, 0)
    for g in range(breadth // LANES):
        here = slice(g * LANES, (g + 1) * LANES)
        out[:, here] = ot[here, :].T


def body(grad_x, grad_y):
    n, m = lax.axis_size("row"), lax.axis_size("col")
    length, breadth = grad_x.shape
    chunk, half, classes = breadth // n, length // 2, 2 * n
    constants = tables(n, m, length, breadth)
    f32, bf16 = jnp.float32, jnp.bfloat16
    size1, size2 = 2 * classes + 8, 2 * classes + -(-n // 8) * 8
    dma = pltpu.SemaphoreType.DMA
    return pl.pallas_call(
        functools.partial(kernel, n, m),
        out_shape=jax.ShapeDtypeStruct((length, breadth), f32),
        in_specs=[pl.BlockSpec(memory_space=pltpu.VMEM)] * 6,
        out_specs=pl.BlockSpec(memory_space=pltpu.VMEM),
        scratch_shapes=[
            pltpu.VMEM((breadth, length), f32),
            pltpu.VMEM((n, chunk, length), f32),
            pltpu.VMEM((8, breadth), f32),
            pltpu.VMEM((8, length), f32),
            pltpu.VMEM((8, length), f32),
            pltpu.VMEM((3 * (n + 1) * 16, length), bf16),
            pltpu.VMEM((3 * n * 16, length), bf16),
            pltpu.VMEM((half // LANES, classes * chunk, LANES), f32),
            pltpu.VMEM((half // LANES, classes * chunk, LANES), f32),
            pltpu.VMEM((size1, half), f32),
            pltpu.VMEM((n, size1, half), f32),
            pltpu.VMEM((size2, half), f32),
            pltpu.VMEM((m, size2, half), f32),
            pltpu.VMEM(((n + 1) * 16, length), f32),
            pltpu.VMEM((n * 16, length), f32),
            pltpu.VMEM((n, chunk, length), f32),
            pltpu.VMEM((breadth, length), f32),
            dma((2,)), dma((2,)),
            dma((chunk // 16, n)), dma((chunk // 16, n)), dma((n,)), dma((n,)),
            dma((m,)), dma((m,)), dma((chunk // 16, n)), dma((chunk // 16, n)),
        ],
        compiler_params=pltpu.CompilerParams(
            collective_id=0, has_side_effects=True, vmem_limit_bytes=60 * 1024 * 1024
        ),
        name="poisson",
    )(grad_x, grad_y, *[jnp.asarray(value) for value in constants])


def solution(mesh):
    placed = (P("row", "col"), P("row", "col"))
    return jax.shard_map(
        body, mesh=mesh, in_specs=placed, out_specs=P("row", "col"), check_vma=False
    )
```

```python
import functools

import jax
import jax.numpy as jnp
import numpy as np
from jax import lax
from jax.experimental import pallas as pl
from jax.experimental.pallas import tpu as pltpu
from jax.sharding import PartitionSpec as P

MESH = pl.DeviceIdType.MESH
LANES = 128


def split3(values):
    first = values.astype(jnp.bfloat16)
    rest = values - first.astype(jnp.float32)
    second = rest.astype(jnp.bfloat16)
    third = (rest - second.astype(jnp.float32)).astype(jnp.bfloat16)
    return first, second, third


def tables(n, cols_members, length, breadth):
    total_x, total_y, chunk, half = n * length, cols_members * breadth, breadth // n, length // 2
    place = np.arange(length)[:, None]
    level = np.arange(half)[None, :]
    phase = ((2 * place + 1) * level) % (2 * length) * (np.pi / length)
    cosine, sine = np.cos(phase), np.sin(phase)
    sine[:, 0] = (-1.0) ** np.arange(length)

    def pieces(table):
        table = table.astype(np.float32)
        kept = []
        for _ in range(3):
            part = table.astype(jnp.bfloat16)
            kept.append(part)
            table = table - part.astype(np.float32)
        return np.stack(kept)

    twist = np.pi * np.arange(n + 1)[:, None] * (2 * np.arange(length)[None, :] + 1) / (2 * total_x)
    turn = np.stack([np.cos(twist), np.sin(twist)]).astype(np.float32)
    freq = np.concatenate(
        [
            np.arange(n + 1)[:, None] + 2 * n * level,
            2 * n * np.where(level == 0, half, level) - np.arange(1, n)[:, None],
        ]
    )
    s = np.sin(np.pi * freq / (2 * total_x))
    c = np.sqrt(1 + s * s)
    zero = freq == 0
    rate = -2 * np.log(c + s)
    decay = lambda count: np.exp(rate * count)
    closing = np.where(zero, 1.0, -np.expm1(np.where(zero, -1.0, rate) * 2 * total_y))
    gain = np.where(zero, 0.0, -2.0 / total_x / np.where(zero, 1.0, 4 * c * s))
    solve = np.stack(
        [
            -np.expm1(rate),
            decay(chunk),
            decay(breadth),
            decay(total_y),
            1 / closing,
            gain,
        ]
    ).astype(np.float32)
    return pieces(cosine), pieces(sine), turn, solve


def weighted(terms):
    total = None
    for coefficient, value in terms:
        if abs(coefficient) < 1e-12:
            continue
        if abs(abs(coefficient) - 1) < 1e-12:
            if total is None:
                total = value if coefficient > 0 else -value
            else:
                total = total + value if coefficient > 0 else total - value
            continue
        part = float(coefficient) * value
        total = part if total is None else total + part
    return total


def kernel(
    n, m, gx_hbm, gy_hbm, cos_hbm, sin_hbm, turn_hbm, solve_hbm, out_hbm,
    gx, gy, cos3, sin3, turn, solve, out, load, leave, dt, recv, hx, hys, hy, s_ref, t_ref, f_ref, u_ref, m1s, m1r, m2s, m2r, sh, th, ob, ot,
    hsend, hrecv, a_send, a_recv, b_send, b_recv, c_send, c_recv, d_send, d_recv,
):
    r, c = lax.axis_index("row"), lax.axis_index("col")
    length, breadth = gx.shape
    chunk, half = breadth // n, length // 2
    tiles, classes = half // LANES, 2 * n
    total_x, total_y = n * length, m * breadth
    pitch = chunk + 1

    loads = [
        pltpu.make_async_copy(source, target, load.at[i])
        for i, (source, target) in enumerate(
            [(gy_hbm, gy), (gx_hbm, gx), (turn_hbm, turn), (cos_hbm, cos3), (sin_hbm, sin3), (solve_hbm, solve)]
        )
    ]
    for copy in loads:
        copy.start()
    barrier = pltpu.get_barrier_semaphore()
    for t in range(1, n):
        pl.semaphore_signal(barrier, inc=1, device_id={"row": lax.rem(r + t, n)}, device_id_type=MESH)
    for t in range(1, m):
        pl.semaphore_signal(barrier, inc=1, device_id={"col": lax.rem(c + t, m)}, device_id_type=MESH)
    pl.semaphore_wait(barrier, n - 1 + m - 1)

    def remote(src, dst, send, recv_sem, axis, who):
        return pltpu.make_async_remote_copy(
            src_ref=src, dst_ref=dst, send_sem=send, recv_sem=recv_sem,
            device_id={axis: who}, device_id_type=MESH,
        )

    loads[0].wait()
    hys[...] = gy[:, breadth - LANES:].T[LANES - 8:]
    halo_y = remote(hys, hy, hsend.at[1], hrecv.at[1], "col", lax.rem(c + 1, m))
    halo_y.start()
    loads[1].wait()
    halo_x = remote(gx.at[pl.ds(length - 8, 8)], hx, hsend.at[0], hrecv.at[0], "row", lax.rem(r + 1, n))
    halo_x.start()
    lane = lax.broadcasted_iota(jnp.int32, (LANES, LANES), 1)
    line = lax.broadcasted_iota(jnp.int32, (LANES, LANES), 0)
    for b in reversed(range(length // LANES)):
        band = slice(b * LANES, (b + 1) * LANES)
        if b == 0:
            halo_x.wait()
            above = hx[7:8, :] * jnp.where(r > 0, 1.0, 0.0)
        for g in range(breadth // LANES):
            here = slice(g * LANES, (g + 1) * LANES)
            x = gx[band, here]
            prior = gx[b * LANES - 1:b * LANES, here] if b else above[:, here]
            up = jnp.where(line == 0, prior, pltpu.roll(x, 1, 0))
            y = gy[band, here]
            edge = pltpu.roll(gy[band, (g - 1) * LANES:g * LANES], 1, 1) if g else 0.0
            left = jnp.where(lane == 0, edge, pltpu.roll(y, 1, 1))
            dt[here, band] = ((x - up) + (y - left)).T
    halo_y.wait()
    top = lax.broadcasted_iota(jnp.int32, (8, length), 0) == 0
    dt[0:8, :] = dt[0:8, :] - jnp.where(top, hy[7:8, :] * jnp.where(c > 0, 1.0, 0.0), 0.0)

    step = 16
    rounds = chunk // step

    def out_piece(i, t):
        who = lax.rem(r + t, n)
        source = pl.multiple_of(who * chunk + i * step, step)
        return remote(
            dt.at[pl.ds(source, step)], recv.at[r, pl.ds(pl.multiple_of(i * step, step), step)],
            a_send.at[i, t], a_recv.at[i, t], "row", who,
        )

    def send_out(i, carry):
        for t in range(1, n):
            out_piece(i, t).start()
        return carry

    lax.fori_loop(0, rounds, send_out, 0)
    recv[r] = dt[pl.ds(pl.multiple_of(r * chunk, chunk), chunk), :]

    depth_s, depth_t = (n + 1) * step, n * step
    ccos = [[np.cos(np.pi * d * p / n) for p in range(n)] for d in range(n + 1)]
    csin = [[np.sin(np.pi * d * p / n) for p in range(n)] for d in range(n + 1)]
    for copy in loads[2:]:
        copy.wait()
    mask = jnp.where(lax.broadcasted_iota(jnp.int32, (step, LANES), 1) == 0, 0.0, 1.0)
    span = lambda i, h: solve[i, :, h * LANES:(h + 1) * LANES]
    fall = [span(0, h) for h in range(tiles)]
    at = lambda j: pl.ds(j, classes, stride=pitch)

    def class_rows(k, i):
        return pl.ds(k * pitch + i * step, step)

    def mix(b):
        rows = pl.ds(pl.multiple_of(b * step, step), step)
        for g in range(length // LANES):
            here = slice(g * LANES, (g + 1) * LANES)
            x = [recv[p, rows, here] for p in range(n)]
            plus = {p: x[p] + x[n - p] for p in range(1, n // 2)}
            minus = {p: x[p] - x[n - p] for p in range(1, n // 2)}
            for d in range(n + 1):
                even = d % 2 == 0
                base = [(1.0, x[0]), (ccos[d][n // 2], x[n // 2])]
                pair, other = (plus, minus) if even else (minus, plus)
                real = weighted(base + [(ccos[d][p], pair[p]) for p in pair])
                imag = weighted([(csin[d][n // 2], x[n // 2])] + [(csin[d][p], other[p]) for p in other])
                if d == 0:
                    s_val = real
                else:
                    co, si = turn[0, d:d + 1, here], turn[1, d:d + 1, here]
                    s_val = co * real if imag is None else co * real - si * imag
                    t_val = si * real if imag is None else si * real + co * imag
                    for i, part in enumerate(split3(t_val)):
                        t_ref[i * depth_t + (d - 1) * step:i * depth_t + d * step, here] = part
                for i, part in enumerate(split3(s_val)):
                    s_ref[i * depth_s + d * step:i * depth_s + (d + 1) * step, here] = part

    def six(a, depth, b):
        dot = functools.partial(jnp.dot, preferred_element_type=jnp.float32)
        one = dot(a[...], b[0])
        two = dot(a[0:2 * depth], b[1])
        small = one[2 * depth:] + two[depth:] + dot(a[0:depth], b[2])
        return one[0:depth] + (one[depth:2 * depth] + two[0:depth] + small)

    def forward(i, carry):
        for t in range(1, n):
            out_piece(i, t).wait_recv()
        mix(i)
        p_all = six(s_ref, depth_s, cos3)
        q_all = six(t_ref, depth_t, sin3)
        for h in range(tiles):
            there = slice(h * LANES, (h + 1) * LANES)
            f_ref[h, class_rows(0, i), :] = p_all[0:step, there]
            for d in range(1, n + 1):
                pd, qd = p_all[d * step:(d + 1) * step, there], q_all[(d - 1) * step:d * step, there]
                f_ref[h, class_rows(d, i), :] = pd - (mask * qd if h == 0 else qd)
                if d < n:
                    f_ref[h, class_rows(n + d, i), :] = (mask * pd if h == 0 else pd) + qd
        ahead, back, power = carry
        for k in range(step):
            f = [f_ref[h, at(i * step + k), :] for h in range(tiles)]
            back = [back[h] + power[h] * f[h] for h in range(tiles)]
            power = [power[h] - fall[h] * power[h] for h in range(tiles)]
            ahead = [(ahead[h] + f[h]) - fall[h] * ahead[h] for h in range(tiles)]
        return ahead, back, power

    nothing = [jnp.zeros((classes, LANES), jnp.float32) for _ in range(tiles)]
    unity = [jnp.ones((classes, LANES), jnp.float32) for _ in range(tiles)]
    ahead, back, _ = lax.fori_loop(0, rounds, forward, (nothing, nothing, unity))
    for h in range(tiles):
        there = slice(h * LANES, (h + 1) * LANES)
        m1s[0:classes, there] = ahead[h]
        m1s[classes:2 * classes, there] = back[h]
    m1s[2 * classes:, :] = jnp.zeros((8, half), jnp.float32)
    m1s[2 * classes:2 * classes + 1, 0:chunk] = f_ref[0, 0:chunk, :].T[0:1, :]
    copies = []
    for t in range(1, n):
        copy = remote(m1s, m1r.at[r], b_send.at[t], b_recv.at[t], "row", lax.rem(r + t, n))
        copy.start()
        copies.append(copy)
    m1r[r] = m1s[...]
    for copy in copies:
        copy.wait()
    grow = solve[1]
    band_a = jnp.zeros((classes, half), jnp.float32)
    band_b = jnp.zeros((classes, half), jnp.float32)
    for p in range(n):
        band_a = grow * band_a + m1r[p, 0:classes, :]
        band_b = grow * band_b + m1r[n - 1 - p, classes:2 * classes, :]
    m2s[0:classes, :] = band_a
    m2s[classes:2 * classes, :] = band_b
    for p in range(n):
        m2s[2 * classes + p:2 * classes + p + 1, :] = m1r[p, 2 * classes:2 * classes + 1, :]
    copies = []
    for t in range(1, m):
        copy = remote(m2s, m2r.at[c], c_send.at[t], c_recv.at[t], "col", lax.rem(c + t, m))
        copy.start()
        copies.append(copy)
    m2r[c] = m2s[...]
    for copy in copies:
        copy.wait()

    wide, whole, close = solve[2], solve[3], solve[4]
    first = jnp.zeros((classes, half), jnp.float32)
    last = jnp.zeros((classes, half), jnp.float32)
    for q in range(m):
        last = wide * last + m2r[q, 0:classes, :]
        first = wide * first + m2r[m - 1 - q, classes:2 * classes, :]
    left_in = (first + whole * last) * close
    right_in = (last + whole * first) * close
    for q in range(m):
        left_in = jnp.where(q < c, wide * left_in + m2r[q, 0:classes, :], left_in)
        right_in = jnp.where(m - 1 - q > c, wide * right_in + m2r[m - 1 - q, classes:2 * classes, :], right_in)
    for p in range(n):
        left_in = jnp.where(p < r, grow * left_in + m1r[p, 0:classes, :], left_in)
        right_in = jnp.where(n - 1 - p > r, grow * right_in + m1r[n - 1 - p, classes:2 * classes, :], right_in)

    me = lax.broadcasted_iota(jnp.int32, (chunk, LANES), 0) + (c * breadth + r * chunk)
    mine = me.astype(jnp.float32)
    mine_sq = mine * (mine + 1.0) * (0.5 / total_y) + (
        (total_y - 1) / 2 - (total_y * total_y - 1) / (6 * total_y)
    )
    column = lax.broadcasted_iota(jnp.int32, (1, LANES), 1).astype(jnp.float32)
    flat = jnp.zeros((chunk, LANES), jnp.float32)
    for q in range(m):
        for p in range(n):
            other = column + float(q * breadth + p * chunk)
            other_sq = other * (other + 1.0) * (0.5 / total_y)
            row = m2r[q, 2 * classes + p:2 * classes + p + 1, 0:LANES]
            flat = flat + (mine_sq + other_sq - jnp.maximum(mine, other)) * row
    constant = jnp.sum(flat, axis=1, keepdims=True) * (-1.0 / total_x)

    gain = [span(5, h) for h in range(tiles)]

    unroll = 8

    def walk(joined):
        def some(b, carry):
            ahead, back = carry
            for k in range(unroll):
                i = b * unroll + k
                j = chunk - 1 - i
                new_ahead, new_back = [], []
                for h in range(tiles):
                    value = (ahead[h] + f_ref[h, at(i), :]) - fall[h] * ahead[h]
                    kept = back[h] - fall[h] * back[h]
                    new_ahead.append(value)
                    new_back.append((back[h] + f_ref[h, at(j), :]) - fall[h] * back[h])
                    if joined:
                        value = gain[h] * (value + u_ref[h, at(i), :])
                        kept = gain[h] * (kept + u_ref[h, at(j), :])
                    u_ref[h, at(i), :] = value
                    u_ref[h, at(j), :] = kept
                ahead, back = new_ahead, new_back
            return ahead, back

        return some

    parts = lambda v: [v[:, h * LANES:(h + 1) * LANES] for h in range(tiles)]
    middle = chunk // 2 // unroll
    state = lax.fori_loop(0, middle, walk(False), (parts(left_in), parts(right_in)))
    lax.fori_loop(middle, 2 * middle, walk(True), state)
    wide_lane = lax.broadcasted_iota(jnp.int32, (chunk, LANES), 1)
    u_ref[0, 0:chunk, :] = jnp.where(wide_lane == 0, constant, u_ref[0, 0:chunk, :])

    def three(a, depth, table):
        dot = lambda x, y: lax.dot_general(
            x, y, (((1,), (1,)), ((), ())), preferred_element_type=jnp.float32
        )
        one = dot(a[0:2 * depth, 0:half], table[0])
        return one[0:depth] + (one[depth:] + dot(a[0:depth, 0:half], table[1]))

    def back_piece(i, t):
        who = lax.rem(r + t, n)
        rows = pl.ds(pl.multiple_of(i * step, step), step)
        home = pl.ds(pl.multiple_of(r * chunk + i * step, step), step)
        return remote(
            ob.at[who, rows], ot.at[home], d_send.at[i, t], d_recv.at[i, t], "row", who
        )

    def inverse(i, carry):
        for h in range(tiles):
            there = slice(h * LANES, (h + 1) * LANES)
            for d in range(n + 1):
                up = u_ref[h, class_rows(d, i), :]
                held = mask * up if h == 0 else up
                if 0 < d < n:
                    um = u_ref[h, class_rows(n + d, i), :]
                    pd, qd = up + (mask * um if h == 0 else um), um - held
                else:
                    pd, qd = up, -held
                for k, part in enumerate(split3(pd)[:2]):
                    s_ref[k * depth_s + d * step:k * depth_s + (d + 1) * step, there] = part
                if d > 0:
                    for k, part in enumerate(split3(qd)[:2]):
                        t_ref[k * depth_t + (d - 1) * step:k * depth_t + d * step, there] = part
        sh[...] = three(s_ref, depth_s, cos3)
        th[...] = three(t_ref, depth_t, sin3)
        rows = pl.ds(pl.multiple_of(i * step, step), step)
        for g in range(length // LANES):
            here = slice(g * LANES, (g + 1) * LANES)
            real, imag = [], []
            for d in range(n + 1):
                s_val = sh[d * step:(d + 1) * step, here]
                if d == 0:
                    real.append(s_val)
                    imag.append(None)
                    continue
                t_val = th[(d - 1) * step:d * step, here]
                co, si = turn[0, d:d + 1, here], turn[1, d:d + 1, here]
                real.append(co * s_val + si * t_val)
                imag.append(co * t_val - si * s_val)
            for p in range(n // 2 + 1):
                evens = weighted([(ccos[d][p], real[d]) for d in range(0, n + 1, 2)])
                odds = weighted([(ccos[d][p], real[d]) for d in range(1, n + 1, 2)])
                if p == 0:
                    ob[0, rows, here] = evens + odds
                    continue
                ievens = weighted([(csin[d][p], imag[d]) for d in range(2, n, 2)])
                iodds = weighted([(csin[d][p], imag[d]) for d in range(1, n, 2)])
                if p == n // 2:
                    ob[p, rows, here] = weighted(
                        [(1.0, v) for v in (evens, odds, ievens, iodds) if v is not None]
                    )
                    continue
                near, far = evens + iodds, odds + ievens
                ob[p, rows, here] = near + far
                ob[n - p, rows, here] = (evens - ievens) + (iodds - odds)
        for t in range(1, n):
            back_piece(i, t).start()
        return carry

    lax.fori_loop(0, rounds, inverse, 0)
    ot[pl.ds(pl.multiple_of(r * chunk, chunk), chunk), :] = ob[r]

    def settle(i, carry):
        for t in range(1, n):
            out_piece(i, t).wait_send()
            back_piece(i, t).wait()
        return carry

    lax.fori_loop(0, rounds, settle, 0)
    for g in range(length // LANES):
        here = slice(g * LANES, (g + 1) * LANES)
        out[here, :] = ot[:, here].T
        pltpu.make_async_copy(out.at[here], out_hbm.at[here], leave.at[g]).start()
    for g in range(length // LANES):
        here = slice(g * LANES, (g + 1) * LANES)
        pltpu.make_async_copy(out.at[here], out_hbm.at[here], leave.at[g]).wait()


def body(grad_x, grad_y):
    n, m = lax.axis_size("row"), lax.axis_size("col")
    length, breadth = grad_x.shape
    chunk, half, classes = breadth // n, length // 2, 2 * n
    constants = tables(n, m, length, breadth)
    f32, bf16 = jnp.float32, jnp.bfloat16
    size1, size2 = 2 * classes + 8, 2 * classes + -(-n // 8) * 8
    dma = pltpu.SemaphoreType.DMA
    return pl.pallas_call(
        functools.partial(kernel, n, m),
        out_shape=jax.ShapeDtypeStruct((length, breadth), f32),
        in_specs=[pl.BlockSpec(memory_space=pl.ANY)] * 6,
        out_specs=pl.BlockSpec(memory_space=pl.ANY),
        scratch_shapes=[
            pltpu.VMEM((length, breadth), f32),
            pltpu.VMEM((length, breadth), f32),
            *[pltpu.VMEM(value.shape, value.dtype) for value in constants],
            pltpu.VMEM((length, breadth), f32),
            dma((6,)),
            dma((length // LANES,)),
            pltpu.VMEM((breadth, length), f32),
            pltpu.VMEM((n, chunk, length), f32),
            pltpu.VMEM((8, breadth), f32),
            pltpu.VMEM((8, length), f32),
            pltpu.VMEM((8, length), f32),
            pltpu.VMEM((3 * (n + 1) * 16, length), bf16),
            pltpu.VMEM((3 * n * 16, length), bf16),
            pltpu.VMEM((half // LANES, classes * (chunk + 1), LANES), f32),
            pltpu.VMEM((half // LANES, classes * (chunk + 1), LANES), f32),
            pltpu.VMEM((size1, half), f32),
            pltpu.VMEM((n, size1, half), f32),
            pltpu.VMEM((size2, half), f32),
            pltpu.VMEM((m, size2, half), f32),
            pltpu.VMEM(((n + 1) * 16, length), f32),
            pltpu.VMEM((n * 16, length), f32),
            pltpu.VMEM((n, chunk, length), f32),
            pltpu.VMEM((breadth, length), f32),
            dma((2,)), dma((2,)),
            dma((chunk // 16, n)), dma((chunk // 16, n)), dma((n,)), dma((n,)),
            dma((m,)), dma((m,)), dma((chunk // 16, n)), dma((chunk // 16, n)),
        ],
        compiler_params=pltpu.CompilerParams(
            collective_id=0, has_side_effects=True, vmem_limit_bytes=60 * 1024 * 1024
        ),
        name="poisson",
    )(grad_x, grad_y, *[jnp.asarray(value) for value in constants])


def solution(mesh):
    placed = (P("row", "col"), P("row", "col"))
    return jax.shard_map(
        body, mesh=mesh, in_specs=placed, out_specs=P("row", "col"), check_vma=False
    )
```

```python
import functools

import jax
import jax.numpy as jnp
import numpy as np
from jax import lax
from jax.experimental import pallas as pl
from jax.experimental.pallas import tpu as pltpu
from jax.sharding import PartitionSpec as P

MESH = pl.DeviceIdType.MESH
LANES = 128


def split3(values):
    first = values.astype(jnp.bfloat16)
    rest = values - first.astype(jnp.float32)
    second = rest.astype(jnp.bfloat16)
    third = (rest - second.astype(jnp.float32)).astype(jnp.bfloat16)
    return first, second, third


def tables(n, cols_members, length, breadth):
    total_x, total_y, chunk, half = n * length, cols_members * breadth, breadth // n, length // 2
    place = np.arange(length)[:, None]
    level = np.arange(half)[None, :]
    phase = ((2 * place + 1) * level) % (2 * length) * (np.pi / length)
    cosine, sine = np.cos(phase), np.sin(phase)
    sine[:, 0] = (-1.0) ** np.arange(length)

    def pieces(table):
        table = table.astype(np.float32)
        kept = []
        for _ in range(3):
            part = table.astype(jnp.bfloat16)
            kept.append(part)
            table = table - part.astype(np.float32)
        return np.stack(kept)

    twist = np.pi * np.arange(n + 1)[:, None] * (2 * np.arange(length)[None, :] + 1) / (2 * total_x)
    turn = np.stack([np.cos(twist), np.sin(twist)]).astype(np.float32)
    freq = np.concatenate(
        [
            np.arange(n + 1)[:, None] + 2 * n * level,
            2 * n * np.where(level == 0, half, level) - np.arange(1, n)[:, None],
        ]
    )
    s = np.sin(np.pi * freq / (2 * total_x))
    c = np.sqrt(1 + s * s)
    zero = freq == 0
    rate = -2 * np.log(c + s)
    decay = lambda count: np.exp(rate * count)
    closing = np.where(zero, 1.0, -np.expm1(np.where(zero, -1.0, rate) * 2 * total_y))
    gain = np.where(zero, 0.0, -2.0 / total_x / np.where(zero, 1.0, 4 * c * s))
    solve = np.stack(
        [
            -np.expm1(rate),
            decay(chunk),
            decay(breadth),
            decay(total_y),
            1 / closing,
            gain,
        ]
    ).astype(np.float32)
    return pieces(cosine), pieces(sine), turn, solve


def weighted(terms):
    total = None
    for coefficient, value in terms:
        if abs(coefficient) < 1e-12:
            continue
        if abs(abs(coefficient) - 1) < 1e-12:
            if total is None:
                total = value if coefficient > 0 else -value
            else:
                total = total + value if coefficient > 0 else total - value
            continue
        part = float(coefficient) * value
        total = part if total is None else total + part
    return total


def kernel(
    n, m, gx_hbm, gy_hbm, cos_hbm, sin_hbm, turn_hbm, solve_hbm, out_hbm,
    gx, gy, cos3, sin3, turn, solve, out, load, leave, dt, recv, hx, hys, hy, s_ref, t_ref, f_ref, u_ref, m1s, m1r, m2s, m2r, sh, th, ob, ot,
    hsend, hrecv, a_send, a_recv, b_send, b_recv, c_send, c_recv, d_send, d_recv,
):
    r, c = lax.axis_index("row"), lax.axis_index("col")
    length, breadth = gx.shape
    chunk, half = breadth // n, length // 2
    tiles, classes = half // LANES, 2 * n
    total_x, total_y = n * length, m * breadth
    pitch = chunk + 1

    loads = [
        pltpu.make_async_copy(source, target, load.at[i])
        for i, (source, target) in enumerate(
            [(gy_hbm, gy), (gx_hbm, gx), (turn_hbm, turn), (cos_hbm, cos3), (sin_hbm, sin3), (solve_hbm, solve)]
        )
    ]
    for copy in loads:
        copy.start()
    barrier = pltpu.get_barrier_semaphore()
    for t in range(1, n):
        pl.semaphore_signal(barrier, inc=1, device_id={"row": lax.rem(r + t, n)}, device_id_type=MESH)
    for t in range(1, m):
        pl.semaphore_signal(barrier, inc=1, device_id={"col": lax.rem(c + t, m)}, device_id_type=MESH)
    pl.semaphore_wait(barrier, n - 1 + m - 1)

    def remote(src, dst, send, recv_sem, axis, who):
        return pltpu.make_async_remote_copy(
            src_ref=src, dst_ref=dst, send_sem=send, recv_sem=recv_sem,
            device_id={axis: who}, device_id_type=MESH,
        )

    loads[0].wait()
    hys[...] = gy[:, breadth - LANES:].T[LANES - 8:]
    halo_y = remote(hys, hy, hsend.at[1], hrecv.at[1], "col", lax.rem(c + 1, m))
    halo_y.start()
    loads[1].wait()
    halo_x = remote(gx.at[pl.ds(length - 8, 8)], hx, hsend.at[0], hrecv.at[0], "row", lax.rem(r + 1, n))
    halo_x.start()
    lane = lax.broadcasted_iota(jnp.int32, (LANES, LANES), 1)
    line = lax.broadcasted_iota(jnp.int32, (LANES, LANES), 0)
    for b in reversed(range(length // LANES)):
        band = slice(b * LANES, (b + 1) * LANES)
        if b == 0:
            halo_x.wait()
            above = hx[7:8, :] * jnp.where(r > 0, 1.0, 0.0)
        for g in range(breadth // LANES):
            here = slice(g * LANES, (g + 1) * LANES)
            x = gx[band, here]
            prior = gx[b * LANES - 1:b * LANES, here] if b else above[:, here]
            up = jnp.where(line == 0, prior, pltpu.roll(x, 1, 0))
            y = gy[band, here]
            edge = pltpu.roll(gy[band, (g - 1) * LANES:g * LANES], 1, 1) if g else 0.0
            left = jnp.where(lane == 0, edge, pltpu.roll(y, 1, 1))
            dt[here, band] = ((x - up) + (y - left)).T
    halo_y.wait()
    top = lax.broadcasted_iota(jnp.int32, (8, length), 0) == 0
    dt[0:8, :] = dt[0:8, :] - jnp.where(top, hy[7:8, :] * jnp.where(c > 0, 1.0, 0.0), 0.0)

    step = 16
    rounds = chunk // step

    def out_piece(i, t):
        who = lax.rem(r + t, n)
        source = pl.multiple_of(who * chunk + i * step, step)
        return remote(
            dt.at[pl.ds(source, step)], recv.at[r, pl.ds(pl.multiple_of(i * step, step), step)],
            a_send.at[i, t], a_recv.at[i, t], "row", who,
        )

    def send_out(i, carry):
        for t in range(1, n):
            out_piece(i, t).start()
        return carry

    lax.fori_loop(0, rounds, send_out, 0)
    recv[r] = dt[pl.ds(pl.multiple_of(r * chunk, chunk), chunk), :]

    depth_s, depth_t = (n + 1) * step, n * step
    ccos = [[np.cos(np.pi * d * p / n) for p in range(n)] for d in range(n + 1)]
    csin = [[np.sin(np.pi * d * p / n) for p in range(n)] for d in range(n + 1)]
    for copy in loads[2:]:
        copy.wait()
    mask = jnp.where(lax.broadcasted_iota(jnp.int32, (step, LANES), 1) == 0, 0.0, 1.0)
    span = lambda i, h: solve[i, :, h * LANES:(h + 1) * LANES]
    fall = [span(0, h) for h in range(tiles)]
    at = lambda j: pl.ds(j, classes, stride=pitch)

    def class_rows(k, i):
        return pl.ds(k * pitch + i * step, step)

    def mix(b):
        rows = pl.ds(pl.multiple_of(b * step, step), step)
        for g in range(length // LANES):
            here = slice(g * LANES, (g + 1) * LANES)
            x = [recv[p, rows, here] for p in range(n)]
            plus = {p: x[p] + x[n - p] for p in range(1, n // 2)}
            minus = {p: x[p] - x[n - p] for p in range(1, n // 2)}
            for d in range(n + 1):
                even = d % 2 == 0
                base = [(1.0, x[0]), (ccos[d][n // 2], x[n // 2])]
                pair, other = (plus, minus) if even else (minus, plus)
                real = weighted(base + [(ccos[d][p], pair[p]) for p in pair])
                imag = weighted([(csin[d][n // 2], x[n // 2])] + [(csin[d][p], other[p]) for p in other])
                if d == 0:
                    s_val = real
                else:
                    co, si = turn[0, d:d + 1, here], turn[1, d:d + 1, here]
                    s_val = co * real if imag is None else co * real - si * imag
                    t_val = si * real if imag is None else si * real + co * imag
                    for i, part in enumerate(split3(t_val)):
                        t_ref[i * depth_t + (d - 1) * step:i * depth_t + d * step, here] = part
                for i, part in enumerate(split3(s_val)):
                    s_ref[i * depth_s + d * step:i * depth_s + (d + 1) * step, here] = part

    def six(a, depth, b):
        dot = functools.partial(jnp.dot, preferred_element_type=jnp.float32)
        one = dot(a[...], b[0])
        two = dot(a[0:2 * depth], b[1])
        small = one[2 * depth:] + two[depth:] + dot(a[0:depth], b[2])
        return one[0:depth] + (one[depth:2 * depth] + two[0:depth] + small)

    def forward(i, carry):
        for t in range(1, n):
            out_piece(i, t).wait_recv()
        mix(i)
        p_all = six(s_ref, depth_s, cos3)
        q_all = six(t_ref, depth_t, sin3)
        for h in range(tiles):
            there = slice(h * LANES, (h + 1) * LANES)
            f_ref[h, class_rows(0, i), :] = p_all[0:step, there]
            for d in range(1, n + 1):
                pd, qd = p_all[d * step:(d + 1) * step, there], q_all[(d - 1) * step:d * step, there]
                f_ref[h, class_rows(d, i), :] = pd - (mask * qd if h == 0 else qd)
                if d < n:
                    f_ref[h, class_rows(n + d, i), :] = (mask * pd if h == 0 else pd) + qd
        ahead, back, power = carry
        for k in range(step):
            f = [f_ref[h, at(i * step + k), :] for h in range(tiles)]
            back = [back[h] + power[h] * f[h] for h in range(tiles)]
            power = [power[h] - fall[h] * power[h] for h in range(tiles)]
            ahead = [(ahead[h] + f[h]) - fall[h] * ahead[h] for h in range(tiles)]
        return ahead, back, power

    nothing = [jnp.zeros((classes, LANES), jnp.float32) for _ in range(tiles)]
    unity = [jnp.ones((classes, LANES), jnp.float32) for _ in range(tiles)]
    ahead, back, _ = lax.fori_loop(0, rounds, forward, (nothing, nothing, unity))
    for h in range(tiles):
        there = slice(h * LANES, (h + 1) * LANES)
        m1s[0:classes, there] = ahead[h]
        m1s[classes:2 * classes, there] = back[h]
    m1s[2 * classes:, :] = jnp.zeros((8, half), jnp.float32)
    m1s[2 * classes:2 * classes + 1, 0:chunk] = f_ref[0, 0:chunk, :].T[0:1, :]
    copies = []
    for t in range(1, n):
        copy = remote(m1s, m1r.at[r], b_send.at[t], b_recv.at[t], "row", lax.rem(r + t, n))
        copy.start()
        copies.append(copy)
    m1r[r] = m1s[...]
    for copy in copies:
        copy.wait()
    grow = solve[1]
    band_a = jnp.zeros((classes, half), jnp.float32)
    band_b = jnp.zeros((classes, half), jnp.float32)
    for p in range(n):
        band_a = grow * band_a + m1r[p, 0:classes, :]
        band_b = grow * band_b + m1r[n - 1 - p, classes:2 * classes, :]
    m2s[0:classes, :] = band_a
    m2s[classes:2 * classes, :] = band_b
    for p in range(n):
        m2s[2 * classes + p:2 * classes + p + 1, :] = m1r[p, 2 * classes:2 * classes + 1, :]
    copies = []
    for t in range(1, m):
        copy = remote(m2s, m2r.at[c], c_send.at[t], c_recv.at[t], "col", lax.rem(c + t, m))
        copy.start()
        copies.append(copy)
    m2r[c] = m2s[...]
    near_a = jnp.zeros((classes, half), jnp.float32)
    near_b = jnp.zeros((classes, half), jnp.float32)
    from_a = jnp.ones((classes, half), jnp.float32)
    from_b = jnp.ones((classes, half), jnp.float32)
    for p in range(n):
        near_a = jnp.where(p < r, grow * near_a + m1r[p, 0:classes, :], near_a)
        from_a = jnp.where(p < r, grow * from_a, from_a)
        near_b = jnp.where(n - 1 - p > r, grow * near_b + m1r[n - 1 - p, classes:2 * classes, :], near_b)
        from_b = jnp.where(n - 1 - p > r, grow * from_b, from_b)
    for copy in copies:
        copy.wait()

    wide, whole, close = solve[2], solve[3], solve[4]
    first = jnp.zeros((classes, half), jnp.float32)
    last = jnp.zeros((classes, half), jnp.float32)
    for q in range(m):
        last = wide * last + m2r[q, 0:classes, :]
        first = wide * first + m2r[m - 1 - q, classes:2 * classes, :]
    left_in = (first + whole * last) * close
    right_in = (last + whole * first) * close
    for q in range(m):
        left_in = jnp.where(q < c, wide * left_in + m2r[q, 0:classes, :], left_in)
        right_in = jnp.where(m - 1 - q > c, wide * right_in + m2r[m - 1 - q, classes:2 * classes, :], right_in)
    left_in = from_a * left_in + near_a
    right_in = from_b * right_in + near_b

    me = lax.broadcasted_iota(jnp.int32, (chunk, LANES), 0) + (c * breadth + r * chunk)
    mine = me.astype(jnp.float32)
    mine_sq = mine * (mine + 1.0) * (0.5 / total_y) + (
        (total_y - 1) / 2 - (total_y * total_y - 1) / (6 * total_y)
    )
    column = lax.broadcasted_iota(jnp.int32, (1, LANES), 1).astype(jnp.float32)
    flat = jnp.zeros((chunk, LANES), jnp.float32)
    for q in range(m):
        for p in range(n):
            other = column + float(q * breadth + p * chunk)
            other_sq = other * (other + 1.0) * (0.5 / total_y)
            row = m2r[q, 2 * classes + p:2 * classes + p + 1, 0:LANES]
            flat = flat + (mine_sq + other_sq - jnp.maximum(mine, other)) * row
    constant = jnp.sum(flat, axis=1, keepdims=True) * (-1.0 / total_x)

    gain = [span(5, h) for h in range(tiles)]

    unroll = 16

    def walk(joined):
        def some(b, carry):
            ahead, back = carry
            for k in range(unroll):
                i = b * unroll + k
                j = chunk - 1 - i
                new_ahead, new_back = [], []
                for h in range(tiles):
                    value = (ahead[h] + f_ref[h, at(i), :]) - fall[h] * ahead[h]
                    kept = back[h] - fall[h] * back[h]
                    new_ahead.append(value)
                    new_back.append((back[h] + f_ref[h, at(j), :]) - fall[h] * back[h])
                    if joined:
                        value = gain[h] * (value + u_ref[h, at(i), :])
                        kept = gain[h] * (kept + u_ref[h, at(j), :])
                    u_ref[h, at(i), :] = value
                    u_ref[h, at(j), :] = kept
                ahead, back = new_ahead, new_back
            return ahead, back

        return some

    parts = lambda v: [v[:, h * LANES:(h + 1) * LANES] for h in range(tiles)]
    middle = chunk // 2 // unroll
    state = lax.fori_loop(0, middle, walk(False), (parts(left_in), parts(right_in)))
    lax.fori_loop(middle, 2 * middle, walk(True), state)
    wide_lane = lax.broadcasted_iota(jnp.int32, (chunk, LANES), 1)
    u_ref[0, 0:chunk, :] = jnp.where(wide_lane == 0, constant, u_ref[0, 0:chunk, :])

    def three(a, depth, table):
        dot = lambda x, y: lax.dot_general(
            x, y, (((1,), (1,)), ((), ())), preferred_element_type=jnp.float32
        )
        one = dot(a[0:2 * depth, 0:half], table[0])
        return one[0:depth] + (one[depth:] + dot(a[0:depth, 0:half], table[1]))

    def back_piece(i, t):
        who = lax.rem(r + t, n)
        rows = pl.ds(pl.multiple_of(i * step, step), step)
        home = pl.ds(pl.multiple_of(r * chunk + i * step, step), step)
        return remote(
            ob.at[who, rows], ot.at[home], d_send.at[i, t], d_recv.at[i, t], "row", who
        )

    def inverse(i, carry):
        for h in range(tiles):
            there = slice(h * LANES, (h + 1) * LANES)
            for d in range(n + 1):
                up = u_ref[h, class_rows(d, i), :]
                held = mask * up if h == 0 else up
                if 0 < d < n:
                    um = u_ref[h, class_rows(n + d, i), :]
                    pd, qd = up + (mask * um if h == 0 else um), um - held
                else:
                    pd, qd = up, -held
                for k, part in enumerate(split3(pd)[:2]):
                    s_ref[k * depth_s + d * step:k * depth_s + (d + 1) * step, there] = part
                if d > 0:
                    for k, part in enumerate(split3(qd)[:2]):
                        t_ref[k * depth_t + (d - 1) * step:k * depth_t + d * step, there] = part
        sh[...] = three(s_ref, depth_s, cos3)
        th[...] = three(t_ref, depth_t, sin3)
        rows = pl.ds(pl.multiple_of(i * step, step), step)
        for g in range(length // LANES):
            here = slice(g * LANES, (g + 1) * LANES)
            real, imag = [], []
            for d in range(n + 1):
                s_val = sh[d * step:(d + 1) * step, here]
                if d == 0:
                    real.append(s_val)
                    imag.append(None)
                    continue
                t_val = th[(d - 1) * step:d * step, here]
                co, si = turn[0, d:d + 1, here], turn[1, d:d + 1, here]
                real.append(co * s_val + si * t_val)
                imag.append(co * t_val - si * s_val)
            for p in range(n // 2 + 1):
                evens = weighted([(ccos[d][p], real[d]) for d in range(0, n + 1, 2)])
                odds = weighted([(ccos[d][p], real[d]) for d in range(1, n + 1, 2)])
                if p == 0:
                    ob[0, rows, here] = evens + odds
                    continue
                ievens = weighted([(csin[d][p], imag[d]) for d in range(2, n, 2)])
                iodds = weighted([(csin[d][p], imag[d]) for d in range(1, n, 2)])
                if p == n // 2:
                    ob[p, rows, here] = weighted(
                        [(1.0, v) for v in (evens, odds, ievens, iodds) if v is not None]
                    )
                    continue
                near, far = evens + iodds, odds + ievens
                ob[p, rows, here] = near + far
                ob[n - p, rows, here] = (evens - ievens) + (iodds - odds)
        for t in range(1, n):
            back_piece(i, t).start()
        return carry

    lax.fori_loop(0, rounds, inverse, 0)
    ot[pl.ds(pl.multiple_of(r * chunk, chunk), chunk), :] = ob[r]

    def settle(i, carry):
        for t in range(1, n):
            out_piece(i, t).wait_send()
            back_piece(i, t).wait()
        return carry

    lax.fori_loop(0, rounds, settle, 0)
    for g in range(length // LANES):
        here = slice(g * LANES, (g + 1) * LANES)
        out[here, :] = ot[:, here].T
        pltpu.make_async_copy(out.at[here], out_hbm.at[here], leave.at[g]).start()
    for g in range(length // LANES):
        here = slice(g * LANES, (g + 1) * LANES)
        pltpu.make_async_copy(out.at[here], out_hbm.at[here], leave.at[g]).wait()


def body(grad_x, grad_y):
    n, m = lax.axis_size("row"), lax.axis_size("col")
    length, breadth = grad_x.shape
    chunk, half, classes = breadth // n, length // 2, 2 * n
    constants = tables(n, m, length, breadth)
    f32, bf16 = jnp.float32, jnp.bfloat16
    size1, size2 = 2 * classes + 8, 2 * classes + -(-n // 8) * 8
    dma = pltpu.SemaphoreType.DMA
    return pl.pallas_call(
        functools.partial(kernel, n, m),
        out_shape=jax.ShapeDtypeStruct((length, breadth), f32),
        in_specs=[pl.BlockSpec(memory_space=pl.ANY)] * 6,
        out_specs=pl.BlockSpec(memory_space=pl.ANY),
        scratch_shapes=[
            pltpu.VMEM((length, breadth), f32),
            pltpu.VMEM((length, breadth), f32),
            *[pltpu.VMEM(value.shape, value.dtype) for value in constants],
            pltpu.VMEM((length, breadth), f32),
            dma((6,)),
            dma((length // LANES,)),
            pltpu.VMEM((breadth, length), f32),
            pltpu.VMEM((n, chunk, length), f32),
            pltpu.VMEM((8, breadth), f32),
            pltpu.VMEM((8, length), f32),
            pltpu.VMEM((8, length), f32),
            pltpu.VMEM((3 * (n + 1) * 16, length), bf16),
            pltpu.VMEM((3 * n * 16, length), bf16),
            pltpu.VMEM((half // LANES, classes * (chunk + 1), LANES), f32),
            pltpu.VMEM((half // LANES, classes * (chunk + 1), LANES), f32),
            pltpu.VMEM((size1, half), f32),
            pltpu.VMEM((n, size1, half), f32),
            pltpu.VMEM((size2, half), f32),
            pltpu.VMEM((m, size2, half), f32),
            pltpu.VMEM(((n + 1) * 16, length), f32),
            pltpu.VMEM((n * 16, length), f32),
            pltpu.VMEM((n, chunk, length), f32),
            pltpu.VMEM((breadth, length), f32),
            dma((2,)), dma((2,)),
            dma((chunk // 16, n)), dma((chunk // 16, n)), dma((n,)), dma((n,)),
            dma((m,)), dma((m,)), dma((chunk // 16, n)), dma((chunk // 16, n)),
        ],
        compiler_params=pltpu.CompilerParams(
            collective_id=0, has_side_effects=True, vmem_limit_bytes=60 * 1024 * 1024
        ),
        name="poisson",
    )(grad_x, grad_y, *[jnp.asarray(value) for value in constants])


def solution(mesh):
    placed = (P("row", "col"), P("row", "col"))
    return jax.shard_map(
        body, mesh=mesh, in_specs=placed, out_specs=P("row", "col"), check_vma=False
    )
```
